32 devices in a mesh: dp: 16 (over z, y, core), seq: 2 (over x).
Axes of the slice: x: 2, y: 2, z: 4, core: 2. Of those that a mesh axis runs over, the one named last changes fastest.
Arguments:
- latents: bfloat16 [2, 16, 1024, 1152], P(None, 'dp', 'seq'), may hold values from -6 to 6
- cond: float32 [24, 1152], replicated, may hold values from -6 to 6
- slot_mask: int32 [2, 16], replicated, may hold values from 0 to 1, as said below
- slot_image: int32 [2, 16], replicated, may hold values from 0 to 23, as said below
- teacher: bfloat16 [2, 16, 1024, 1152], P(None, 'dp', 'seq'), may hold values from -6 to 6
- cotangent: bfloat16 [2, 16, 1024, 1152], P(None, 'dp', 'seq'), may hold values from -6 to 6
- ada_w: bfloat16 [1152, 6912], P('dp', 'seq'), may hold values from -0.1875 to 0.1875
- ada_b: float32 [6912], replicated, may hold values from -3 to 3
- qkv_w: bfloat16 [1152, 3456], P('dp', 'seq'), may hold values from -0.1875 to 0.1875
- qv_b: float32 [2304], replicated, may hold values from -2 to 2
- proj_w: bfloat16 [1152, 1152], P('dp', 'seq'), may hold values from -1.5 to 1.5
- proj_b: float32 [1152], replicated, may hold values from -2 to 2
- fc1_w: bfloat16 [1152, 4608], P('dp', 'seq'), may hold values from -0.1875 to 0.1875
- fc1_b: float32 [4608], replicated, may hold values from -2 to 2
- fc2_w: bfloat16 [4608, 1152], P('dp', 'seq'), may hold values from -0.09375 to 0.09375
- fc2_b: float32 [1152], replicated, may hold values from -2 to 2
Outputs:
- block_out: bfloat16 [2, 16, 1024, 1152], P(None, 'dp', 'seq')
- latents_grad: float32 [2, 16, 1024, 1152], P(None, 'dp', 'seq')
- loss: float32 [], replicated
- cond_grad: float32 [24, 1152], replicated
- ada_w_grad: float32 [1152, 6912], P('dp', 'seq')
- ada_b_grad: float32 [6912], replicated
- qkv_w_grad: float32 [1152, 3456], P('dp', 'seq')
- qv_b_grad: float32 [2304], replicated
- proj_w_grad: float32 [1152, 1152], P('dp', 'seq')
- proj_b_grad: float32 [1152], replicated
- fc1_w_grad: float32 [1152, 4608], P('dp', 'seq')
- fc1_b_grad: float32 [4608], replicated
- fc2_w_grad: float32 [4608, 1152], P('dp', 'seq')
- fc2_b_grad: float32 [1152], replicated
The draws below stay inside these ranges and needn't reach their ends.
Inputs may be any that keep to these rules, and one draw needn't show every extreme that they name: Micro-batch i holds the images n with n mod 2 = i, each in exactly one slot with slot_mask 1; all other slots have slot_mask 0. `slot_image`: in a slot with slot_mask 1, the image it holds; in a pad slot any image number.
All inputs are finite; a program needn't handle non-finite values.
Results may differ from the reference program's by a relative error of at most 0.018.
The reference program's roundings to bfloat16 on the way count: a program that leaves them out, or rounds other values in their place, can miss the bound.
Values may be sent and summed in bfloat16 or wider, within the bound.
A program may use at most 448 MiB of HBM per device.

```python
import jax
import jax.numpy as jnp
from jax import lax

D = 1152
HEADS = 16
HEAD = 72
FF = 4608
LEN = 1024
MICRO = 2
SLOTS = 16
IMAGES = 24


def slot_layout(key):
    base = jax.random.fold_in(key, 11)
    numbers = jnp.arange(IMAGES, dtype=jnp.int32)
    batch_of = numbers % MICRO
    rank_of = numbers // MICRO
    orders = jax.vmap(lambda sub: jax.random.permutation(sub, SLOTS))(jax.random.split(base, MICRO))
    places = orders[batch_of, rank_of].astype(jnp.int32)
    filled = jnp.zeros((MICRO, SLOTS), jnp.int32).at[batch_of, places].set(1)
    filler = jax.random.randint(jax.random.fold_in(base, 1), (MICRO, SLOTS), 0, IMAGES).astype(jnp.int32)
    holder = filler.at[batch_of, places].set(numbers)
    return (filled, holder)


def draw_slot_mask(key, part):
    filled, holder = slot_layout(key)
    return filled


def draw_slot_image(key, part):
    filled, holder = slot_layout(key)
    return holder


def levels(rng, dims, cuts, smallest, top_value):
    gain, own = 1.0, jax.random.fold_in(rng, 6)
    for position, blocks in cuts:
        heights = jnp.exp(jax.random.uniform(jax.random.fold_in(own, position), (blocks,), jnp.float32, smallest / len(cuts), top_value / len(cuts)))
        gain = gain * jnp.repeat(heights, dims[position] // blocks).reshape([-1 if axis == position else 1 for axis in range(len(dims))])
    return gain


def noise(key, extent, scale, reach, shards=(), kind=jnp.bfloat16):
    values = jax.random.normal(key, extent, jnp.float32) * scale
    if len(shards) > 0:
        values = levels(key, extent, shards, -0.22, 0.18) * values
    return jnp.clip(values, min=-reach, max=reach).astype(kind)


def setup_inputs(seed: int = 0) -> dict:
    splits = jax.random.split(jax.random.key(seed), 17)
    latents = noise(splits[0], (MICRO, SLOTS, LEN, D), 1.0, 6.0, ((1, 16), (2, 2)))
    cond = noise(splits[1], (IMAGES, D), 1.0, 6.0, (), jnp.float32)
    slot_mask = draw_slot_mask(jax.random.fold_in(splits[16], 71), 0)
    slot_image = draw_slot_image(jax.random.fold_in(splits[16], 71), 0)
    teacher = noise(splits[4], (MICRO, SLOTS, LEN, D), 1.0, 6.0, ((1, 16), (2, 2)))
    cotangent = noise(splits[5], (MICRO, SLOTS, LEN, D), 1.0, 6.0, ((1, 16), (2, 2)))
    ada_w = noise(splits[6], (D, 6 * D), D ** -0.5, 0.1875, ((0, 16), (1, 2)))
    ada_b = noise(splits[7], (6 * D,), 0.5, 3.0, (), jnp.float32)
    qkv_w = noise(splits[8], (D, 3 * D), D ** -0.5, 0.1875, ((0, 16), (1, 2)))
    qv_b = noise(splits[9], (2 * D,), 0.3, 2.0, (), jnp.float32)
    proj_w = noise(splits[10], (D, D), (max(D // 64, 4)) ** -0.5, 1.5, ((0, 16), (1, 2)))
    proj_b = noise(splits[11], (D,), 0.3, 2.0, (), jnp.float32)
    fc1_w = noise(splits[12], (D, FF), D ** -0.5, 0.1875, ((0, 16), (1, 2)))
    fc1_b = noise(splits[13], (FF,), 0.3, 2.0, (), jnp.float32)
    fc2_w = noise(splits[14], (FF, D), FF ** -0.5, 0.09375, ((0, 16), (1, 2)))
    fc2_b = noise(splits[15], (D,), 0.3, 2.0, (), jnp.float32)
    return dict(latents=latents, cond=cond, slot_mask=slot_mask, slot_image=slot_image, teacher=teacher, cotangent=cotangent, ada_w=ada_w, ada_b=ada_b, qkv_w=qkv_w, qv_b=qv_b, proj_w=proj_w, proj_b=proj_b, fc1_w=fc1_w, fc1_b=fc1_b, fc2_w=fc2_w, fc2_b=fc2_b)


@jax.custom_vjp
def low(v):
    return lax.optimization_barrier(v.astype(jnp.bfloat16)).astype(jnp.float32)

@jax.custom_vjp
def low_back(v):
    return v

def low_keep(v):
    return (low(v), None)

def low_pass(kept, grad):
    return (grad,)

def back_keep(v):
    return (v, None)

def back_low(kept, grad):
    return (low(grad),)
low.defvjp(low_keep, low_pass)
low_back.defvjp(back_keep, back_low)
HIGH = lax.Precision.HIGHEST

def layer_norm(value):
    center = value - lax.optimization_barrier(jnp.mean(value, axis=-1, keepdims=True))
    spread = lax.optimization_barrier(jnp.mean(center * center, axis=-1, keepdims=True))
    return center * lax.rsqrt(spread + 1e-06)

def attention(query, keys, values):
    group = query.shape[0]
    block = min(512, LEN)
    blocks = LEN // block
    scale = HEAD ** (-0.5)
    query_blocks = query.reshape(group, blocks, block, HEADS, HEAD).transpose(1, 0, 2, 3, 4)

    def one_block(query_block):
        scores = jnp.einsum('gqhe,gkhe->ghqk', query_block, keys, precision=HIGH) * scale
        scores = low_back(scores)
        probs = low(jax.nn.softmax(scores, axis=-1))
        return jnp.einsum('ghqk,gkhe->gqhe', probs, values, precision=HIGH)
    outputs = lax.map(jax.checkpoint(one_block), query_blocks)
    return outputs.transpose(1, 0, 2, 3, 4).reshape(group, LEN, D)

def block_forward(latent_in, cond_in, images, weights):
    ada_w, ada_b, qkv_w, qv_b, proj_w, proj_b, fc1_w, fc1_b, fc2_w, fc2_b = weights
    group = latent_in.shape[0]
    cond_rows = cond_in[images]
    silu_cond = low(jax.nn.silu(cond_rows))
    modulation = low_back(jnp.dot(silu_cond, ada_w, precision=HIGH) + ada_b)
    pieces = [modulation[:, index * D:(index + 1) * D][:, None, :] for index in range(6)]
    shift1, scale1, gate1, shift2, scale2, gate2 = pieces
    hidden = low(layer_norm(latent_in) * (1.0 + scale1) + shift1)
    joint = jnp.einsum('gtd,de->gte', hidden, qkv_w, precision=HIGH)
    query = low_back(low(joint[..., :D] + qv_b[:D]))
    keys = low_back(low(joint[..., D:2 * D]))
    values = low_back(low(joint[..., 2 * D:] + qv_b[D:]))
    attended = attention(query.reshape(group, LEN, HEADS, HEAD), keys.reshape(group, LEN, HEADS, HEAD), values.reshape(group, LEN, HEADS, HEAD))
    attended = low_back(low(attended))
    branch = low_back(jnp.einsum('gtd,de->gte', attended, proj_w, precision=HIGH) + proj_b)
    middle = latent_in + gate1 * branch
    hidden2 = low(layer_norm(middle) * (1.0 + scale2) + shift2)
    before = low_back(jnp.einsum('gtd,df->gtf', hidden2, fc1_w, precision=HIGH) + fc1_b)
    active = low(jax.nn.gelu(before, approximate=True))
    mlp_out = low_back(jnp.einsum('gtf,fd->gtd', active, fc2_w, precision=HIGH) + fc2_b)
    return middle + gate2 * mlp_out

def reference(latents, cond, slot_mask, slot_image, teacher, cotangent, ada_w, ada_b, qkv_w, qv_b, proj_w, proj_b, fc1_w, fc1_b, fc2_w, fc2_b):
    group = 4
    rounds = MICRO * SLOTS // group
    count = jnp.sum(slot_mask).astype(jnp.float32) * LEN
    divisor = count * D
    params = tuple((w.astype(jnp.float32) for w in (ada_w, ada_b, qkv_w, qv_b, proj_w, proj_b, fc1_w, fc1_b, fc2_w, fc2_b)))
    latent_rounds = latents.reshape(rounds, group, LEN, D)
    teacher_rounds = teacher.reshape(rounds, group, LEN, D)
    cot_rounds = cotangent.reshape(rounds, group, LEN, D)
    mask_rounds = slot_mask.reshape(rounds, group)
    image_rounds = slot_image.reshape(rounds, group).astype(jnp.int32)

    def one_round(carry, item):
        sums, loss_sum = carry
        latent_part, teacher_part, cot_part, mask_part, image_part = item

        def forward(latent_in, cond_in, *weights):
            return block_forward(latent_in, cond_in, image_part, weights)
        result, pull = jax.vjp(forward, latent_part.astype(jnp.float32), cond, *params)
        valid = mask_part.astype(jnp.float32)[:, None, None]
        diff = result - teacher_part.astype(jnp.float32)
        loss_sum = loss_sum + jnp.sum(valid * diff * diff)
        grad_out = valid * (2.0 * diff / divisor + cot_part.astype(jnp.float32))
        grads = pull(grad_out)
        sums = tuple((a + b for a, b in zip(sums, grads[1:])))
        return ((sums, loss_sum), (result.astype(jnp.bfloat16), grads[0]))
    start = (tuple((jnp.zeros_like(p) for p in (cond,) + params)), jnp.zeros((), jnp.float32))
    (sums, loss_sum), (outs, latent_grads) = lax.scan(one_round, start, (latent_rounds, teacher_rounds, cot_rounds, mask_rounds, image_rounds))
    block_out = outs.reshape(MICRO, SLOTS, LEN, D)
    latents_grad = latent_grads.reshape(MICRO, SLOTS, LEN, D)
    loss = loss_sum / divisor
    return (block_out, latents_grad, loss, sums[0], sums[1], sums[2], sums[3], sums[4], sums[5], sums[6], sums[7], sums[8], sums[9], sums[10])
```

```python
import functools

import jax
import jax.numpy as jnp
from jax import lax
from jax.experimental import pallas as pl
from jax.experimental.pallas import tpu as pltpu
from jax.sharding import PartitionSpec as P

HEADS = 16
HIGH = lax.Precision.HIGHEST
LOG2E = 1.4426950408889634
F32 = jnp.float32
BF16 = jnp.bfloat16
NT = (((1,), (1,)), ((), ()))
NN = (((1,), (0,)), ((), ()))
TN = (((0,), (0,)), ((), ()))


def dot(a, b, dims=NN):
    return lax.dot_general(a, b, dims, preferred_element_type=F32)


def params(**kw):
    return pltpu.CompilerParams(vmem_limit_bytes=56 * 2**20, **kw)


def attn_fwd_kernel(heads, hs, coef, q_ref, kv_ref, o_ref, lse_ref, qs, ks, vt, os):
    width = heads * hs
    for h in range(heads):
        cols = slice(h * hs, (h + 1) * hs)
        qs[h] = q_ref[0, :, cols]
        ks[h] = kv_ref[0, :, cols]
        vt[h] = kv_ref[0, :, width + h * hs : width + (h + 1) * hs].T

    def head(h, carry):
        scores = dot(ks[h], qs[h], NT)
        top = jnp.max(scores, axis=0, keepdims=True)
        probs = jnp.exp2((scores - top) * coef)
        total = jnp.sum(probs, axis=0, keepdims=True)
        out = dot(vt[h], probs.astype(BF16)) / total
        os[h] = out.T.astype(BF16)
        lse_ref[0, h] = top * coef + jnp.log2(total)
        return carry

    lax.fori_loop(0, heads, head, 0)
    for h in range(heads):
        o_ref[0, :, h * hs : (h + 1) * hs] = os[h]


def attn_fwd(q, kv, heads):
    batch, lq, width = q.shape
    lk = kv.shape[1]
    hs = width // heads
    return pl.pallas_call(
        functools.partial(attn_fwd_kernel, heads, hs, hs**-0.5 * LOG2E),
        grid=(batch,),
        in_specs=[
            pl.BlockSpec((1, lq, width), lambda b: (b, 0, 0)),
            pl.BlockSpec((1, lk, 2 * width), lambda b: (b, 0, 0)),
        ],
        out_specs=[
            pl.BlockSpec((1, lq, width), lambda b: (b, 0, 0)),
            pl.BlockSpec((1, heads, 1, lq), lambda b: (b, 0, 0, 0)),
        ],
        out_shape=[
            jax.ShapeDtypeStruct((batch, lq, width), BF16),
            jax.ShapeDtypeStruct((batch, heads, 1, lq), F32),
        ],
        scratch_shapes=[
            pltpu.VMEM((heads, lq, hs), BF16),
            pltpu.VMEM((heads, lk, hs), BF16),
            pltpu.VMEM((heads, hs, lk), BF16),
            pltpu.VMEM((heads, lq, hs), BF16),
        ],
        compiler_params=params(),
        cost_estimate=pl.CostEstimate(
            flops=4 * batch * lq * lk * width,
            transcendentals=batch * heads * lq * lk,
            bytes_accessed=batch * width * (4 * lq + 4 * lk),
        ),
        name="attn_fwd",
    )(q, kv)


def attn_bwd_kernel(
    heads, hs, coef, scale, q_ref, kv_ref, do_ref, lse_ref, dq_ref, dkv_ref, qs, ks, kt, vs, ds, dks, dvs
):
    width = heads * hs
    for h in range(heads):
        cols = slice(h * hs, (h + 1) * hs)
        qs[h] = q_ref[0, :, cols]
        ds[h] = do_ref[0, :, cols]
        key = kv_ref[0, :, cols]
        ks[h] = key
        kt[h] = key.T
        vs[h] = kv_ref[0, :, width + h * hs : width + (h + 1) * hs]

    def head(h, carry):
        query, grad = qs[h], ds[h]
        probs = jnp.exp2(dot(ks[h], query, NT) * coef - lse_ref[0, h])
        dvs[h] = dot(probs.astype(BF16), grad).astype(BF16)
        weighted = probs * dot(vs[h], grad, NT)
        inner = jnp.sum(weighted, axis=0, keepdims=True)
        dscore = (weighted - probs * inner).astype(BF16)
        dks[h] = (dot(dscore, query) * scale).astype(BF16)
        qs[h] = (dot(kt[h], dscore) * scale).T.astype(BF16)
        return carry

    lax.fori_loop(0, heads, head, 0)
    for h in range(heads):
        cols = slice(h * hs, (h + 1) * hs)
        dq_ref[0, :, cols] = qs[h]
        dkv_ref[0, :, cols] = dks[h]
        dkv_ref[0, :, width + h * hs : width + (h + 1) * hs] = dvs[h]


def attn_bwd(q, kv, grad, lse, heads):
    batch, lq, width = q.shape
    lk = kv.shape[1]
    hs = width // heads
    row = pl.BlockSpec((1, lq, width), lambda b: (b, 0, 0))
    wide = pl.BlockSpec((1, lk, 2 * width), lambda b: (b, 0, 0))
    return pl.pallas_call(
        functools.partial(attn_bwd_kernel, heads, hs, hs**-0.5 * LOG2E, hs**-0.5),
        grid=(batch,),
        in_specs=[row, wide, row, pl.BlockSpec((1, heads, 1, lq), lambda b: (b, 0, 0, 0))],
        out_specs=[row, wide],
        out_shape=[
            jax.ShapeDtypeStruct((batch, lq, width), BF16),
            jax.ShapeDtypeStruct((batch, lk, 2 * width), BF16),
        ],
        scratch_shapes=[
            pltpu.VMEM((heads, lq, hs), BF16),
            pltpu.VMEM((heads, lk, hs), BF16),
            pltpu.VMEM((heads, hs, lk), BF16),
            pltpu.VMEM((heads, lk, hs), BF16),
            pltpu.VMEM((heads, lq, hs), BF16),
            pltpu.VMEM((heads, lk, hs), BF16),
            pltpu.VMEM((heads, lk, hs), BF16),
        ],
        compiler_params=params(),
        cost_estimate=pl.CostEstimate(
            flops=10 * batch * lq * lk * width,
            transcendentals=batch * heads * lq * lk,
            bytes_accessed=batch * width * (8 * lq + 8 * lk),
        ),
        name="attn_bwd",
    )(q, kv, grad, lse)


def norm_parts(value):
    center = value - jnp.mean(value, axis=-1, keepdims=True)
    spread = jnp.mean(center * center, axis=-1, keepdims=True)
    inv = lax.rsqrt(spread + 1e-06)
    return center * inv, inv


def norm_grad(normed, inv, grad):
    first = jnp.mean(grad, axis=-1, keepdims=True)
    second = jnp.mean(grad * normed, axis=-1, keepdims=True)
    return inv * (grad - first - normed * second)


def gelu_tanh(value):
    return jax.nn.gelu(value, approximate=True)


def scatter(grad):
    rows = lax.psum_scatter(grad.astype(BF16), "dp", scatter_dimension=0, tiled=True)
    return lax.psum_scatter(rows, "seq", scatter_dimension=1, tiled=True).astype(F32)


def gather(weight):
    return lax.all_gather(
        lax.all_gather(weight, "seq", axis=1, tiled=True), "dp", axis=0, tiled=True
    )


def local(
    latents,
    cond,
    slot_mask,
    slot_image,
    teacher,
    cotangent,
    ada_w,
    ada_b,
    qkv_w,
    qv_b,
    proj_w,
    proj_b,
    fc1_w,
    fc1_b,
    fc2_w,
    fc2_b,
):
    micro, slots_dev, length, width = latents.shape
    images = cond.shape[0]
    nd, ns = lax.axis_size("dp"), lax.axis_size("seq")
    dp_index, seq_index = lax.axis_index("dp"), lax.axis_index("seq")
    batch = micro * slots_dev
    tokens = batch * length
    full = length * ns
    rows_dev, mod_cols = ada_w.shape
    count = jnp.sum(slot_mask).astype(F32) * full
    divisor = count * width

    lat = latents.reshape(batch, length, width)
    lat_all = lax.all_gather(lat, "seq", axis=1, tiled=True)
    qkv = gather(qkv_w)
    proj = gather(proj_w)
    fc1 = gather(fc1_w)
    fc2 = gather(fc2_w)

    image_table = jnp.arange(images, dtype=jnp.int32)
    by_dev = slot_image.reshape(micro, nd, slots_dev).transpose(1, 0, 2).reshape(nd * batch)
    pick = (by_dev[:, None] == image_table[None, :]).astype(F32)
    cond_all = jnp.dot(pick, cond, precision=HIGH)
    cond_own = lax.dynamic_slice_in_dim(cond_all, dp_index * rows_dev, rows_dev, 1)
    silu_own = jax.nn.silu(cond_own).astype(BF16)
    mod_part = lax.psum_scatter(dot(silu_own, ada_w), "dp", scatter_dimension=0, tiled=True)
    modulation = lax.all_gather(mod_part, "seq", axis=1, tiled=True) + ada_b
    pieces = [modulation[:, i * width : (i + 1) * width][:, None, :] for i in range(6)]
    shift1, scale1, gate1, shift2, scale2, gate2 = pieces

    normed_all, inv_all = norm_parts(lat_all.astype(F32))
    hidden_all = (normed_all * (1.0 + scale1) + shift1).astype(BF16)
    own = lambda value: lax.dynamic_slice_in_dim(value, seq_index * length, length, 1)
    hidden = own(hidden_all)
    inputs = lat.astype(F32)
    flat = lambda value: value.reshape(-1, value.shape[-1])
    wide = lambda value: value.reshape(batch, -1, value.shape[-1])

    query = (dot(flat(hidden), qkv[:, :width]) + qv_b[:width]).astype(BF16)
    kv_bias = jnp.concatenate([jnp.zeros((width,), F32), qv_b[width:]])
    kv = (dot(flat(hidden_all), qkv[:, width:]) + kv_bias).astype(BF16)
    query, kv = wide(query), wide(kv)
    attended, lse = attn_fwd(query, kv, HEADS)

    branch = wide(dot(flat(attended), proj) + proj_b)
    middle = inputs + gate1 * branch
    normed2, inv2 = norm_parts(middle)
    hidden2 = flat((normed2 * (1.0 + scale2) + shift2).astype(BF16))
    before = dot(hidden2, fc1) + fc1_b
    active = gelu_tanh(before).astype(BF16)
    mlp_out = wide(dot(active, fc2) + fc2_b)
    result = middle + gate2 * mlp_out
    block_out = result.astype(BF16).reshape(latents.shape)

    mask_mine = lax.dynamic_slice_in_dim(slot_mask, dp_index * slots_dev, slots_dev, 1)
    valid = mask_mine.reshape(batch, 1, 1).astype(F32)
    diff = result - teacher.reshape(lat.shape).astype(F32)
    loss_sum = jnp.sum(valid * diff * diff)
    grad_out = valid * (2.0 * diff / divisor + cotangent.reshape(lat.shape).astype(F32))
    d_gate2 = jnp.sum(grad_out * mlp_out, axis=1)
    d_mlp = flat((grad_out * gate2).astype(BF16))
    grad_fc2 = dot(active, d_mlp, TN)
    fc2_w_grad = scatter(grad_fc2)
    bias_fc2 = jnp.sum(d_mlp.astype(F32), axis=0)
    d_active = dot(d_mlp, fc2, NT)
    d_before = jax.vjp(gelu_tanh, before)[1](d_active)[0].astype(BF16)
    grad_fc1 = dot(hidden2, d_before, TN)
    fc1_w_grad = scatter(grad_fc1)
    bias_fc1 = jnp.sum(d_before.astype(F32), axis=0)
    d_hidden2 = wide(dot(d_before, fc1, NT))
    d_scale2 = jnp.sum(d_hidden2 * normed2, axis=1)
    d_shift2 = jnp.sum(d_hidden2, axis=1)
    d_middle = grad_out + norm_grad(normed2, inv2, d_hidden2 * (1.0 + scale2))
    d_gate1 = jnp.sum(d_middle * branch, axis=1)
    d_branch = flat((d_middle * gate1).astype(BF16))
    grad_proj = dot(flat(attended), d_branch, TN)
    proj_w_grad = scatter(grad_proj)
    bias_proj = jnp.sum(d_branch.astype(F32), axis=0)
    d_attended = wide(dot(d_branch, proj, NT).astype(BF16))

    d_query, d_kv = attn_bwd(query, kv, d_attended, lse, HEADS)
    d_query, d_kv = flat(d_query), flat(d_kv)
    grad_q = dot(flat(hidden), d_query, TN)
    grad_kv = dot(flat(hidden_all), d_kv, TN)
    qkv_w_grad = scatter(jnp.concatenate([grad_q, grad_kv], axis=1))
    bias_qv = jnp.concatenate(
        [jnp.sum(d_query.astype(F32), axis=0), jnp.sum(d_kv[:, width:].astype(F32), axis=0)]
    )
    dh_q = wide(dot(d_query, qkv[:, :width], NT))
    dh_kv = wide(dot(d_kv, qkv[:, width:], NT))
    others = lax.psum_scatter(dh_kv.astype(BF16), "seq", scatter_dimension=1, tiled=True)
    d_hidden = dh_q + others.astype(F32)
    normed1, inv1 = own(normed_all), own(inv_all)
    d_scale1 = jnp.sum(dh_kv * normed_all, axis=1) + jnp.sum(dh_q * normed1, axis=1)
    d_shift1 = jnp.sum(dh_kv, axis=1) + jnp.sum(dh_q, axis=1)
    d_inputs = d_middle + norm_grad(normed1, inv1, d_hidden * (1.0 + scale1))
    latents_grad = d_inputs.reshape(latents.shape)

    mod_partial = jnp.concatenate([d_shift1, d_scale1, d_gate1, d_shift2, d_scale2, d_gate2], axis=-1)
    d_mod = lax.psum(mod_partial, "seq").astype(BF16)
    col_start = seq_index * mod_cols
    own_cols = lax.dynamic_slice_in_dim(d_mod, col_start, mod_cols, 1)
    d_mod_all = lax.all_gather(own_cols, "dp", axis=0, tiled=True)
    ada_w_grad = dot(silu_own, d_mod_all, TN)
    bias_ada = lax.dynamic_update_slice(
        jnp.zeros((6 * width,), F32), jnp.sum(own_cols.astype(F32), axis=0), (col_start,)
    )
    d_cond = dot(d_mod_all, ada_w, NT)
    d_cond = jax.vjp(jax.nn.silu, cond_own)[1](d_cond)[0]
    grad_cond = lax.dynamic_update_slice(
        jnp.zeros((images, width), F32),
        lax.dot_general(pick, d_cond, TN, precision=HIGH),
        (0, dp_index * rows_dev),
    )
    summed = lax.psum(
        (loss_sum, bias_ada, bias_qv, bias_proj, bias_fc1, bias_fc2, grad_cond), ("dp", "seq")
    )
    return (
        block_out,
        latents_grad,
        summed[0] / divisor,
        summed[6],
        ada_w_grad,
        summed[1],
        qkv_w_grad,
        summed[2],
        proj_w_grad,
        summed[3],
        fc1_w_grad,
        summed[4],
        fc2_w_grad,
        summed[5],
    )


def solution(mesh):
    tokens = P(None, "dp", "seq", None)
    both = P("dp", "seq")
    return jax.shard_map(
        local,
        mesh=mesh,
        in_specs=(tokens, P(), P(), P(), tokens, tokens, both, P(), both, P(), both, P(), both, P(), both, P()),
        out_specs=(tokens, tokens, P(), P(), both, P(), both, P(), both, P(), both, P(), both, P()),
        check_vma=False,
    )
```
